32 devices in a mesh: dp: 8 (over y, x, core), space: 4 (over z).
Axes of the slice: x: 2, y: 2, z: 4, core: 2. Of those that a mesh axis runs over, the one named last changes fastest.
Arguments:
- inputs: bfloat16 [8, 4, 4, 8, 8, 128], P('dp', 'space'), may hold values from -6 to 6
- pre_act: bfloat16 [8, 4, 16, 8, 8, 128], P('dp', 'space'), may hold values from -6 to 6
- out_grad: bfloat16 [8, 8, 32, 16, 256], P('dp', 'space'), may hold values from -6 to 6
- conv1_weight: bfloat16 [27, 4, 16], replicated, may hold values from -0.3125 to 0.3125
- conv2_weight: bfloat16 [27, 16, 32], replicated, may hold values from -0.21875 to 0.21875
Outputs:
- input_grad: bfloat16 [8, 4, 4, 8, 8, 128], P('dp', 'space')
- conv1_grad: float32 [27, 4, 16], replicated
- conv2_grad: float32 [27, 16, 32], replicated
The draws below stay inside these ranges and needn't reach their ends.
All inputs are finite; a program needn't handle non-finite values.
Results may differ from the reference program's by a relative error of at most 0.0049.
Values may be sent and summed in bfloat16 or wider, within the bound.
A program may use at most 64 MiB of HBM per device.

```python
import jax
import jax.numpy as jnp
from jax import lax

C0 = 4
C1 = 16
C2 = 32
DZ = 8
TH = 8
TW = 128
TILES = 4
H = 16
W = 256
VOLUMES = 8
N_SPACE = 4


def levels(own_key, dims, pieces, smallest, largest):
    def one(position, shards_of):
        draws = jax.random.uniform(jax.random.fold_in(jax.random.fold_in(own_key, 6), position), (shards_of,), jnp.float32, smallest / len(pieces), largest / len(pieces))
        return jnp.repeat(jnp.exp(draws), dims[position] // shards_of).reshape((-1,) + (1,) * (len(dims) - position - 1))

    gain = one(*pieces[0])
    for cut in pieces[1:]:
        gain = gain * one(*cut)
    return gain


def gaussian(stream_key, shape, spread, reach, pieces=(), kind=jnp.bfloat16):
    values = spread * jax.random.normal(stream_key, shape, jnp.float32)
    if pieces:
        values = values * levels(stream_key, shape, pieces, -0.22, 0.18)
    return jnp.clip(values, -reach, reach).astype(kind)


def setup_inputs(seed: int = 0) -> dict:
    key_of = jax.random.split(jax.random.key(seed), 6)
    return {
        "inputs": gaussian(key_of[0], (VOLUMES, TILES, C0, DZ, TH, TW), 1.0, 6.0, ((0, 8), (1, 4))),
        "pre_act": gaussian(key_of[1], (VOLUMES, TILES, C1, DZ, TH, TW), 1.0, 6.0, ((0, 8), (1, 4))),
        "out_grad": gaussian(key_of[2], (VOLUMES, DZ, C2, H, W), 1.0, 6.0, ((0, 8), (1, 4))),
        "conv1_weight": gaussian(key_of[3], (27, C0, C1), (27 * C1) ** -0.5, 0.3125),
        "conv2_weight": gaussian(key_of[4], (27, C1, C2), (27 * C2) ** -0.5, 0.21875),
    }


leak = 0.3
numbers = ('NCDHW', 'OIDHW', 'NCDHW')

def whole_volume(tiles):
    tile_cols = N_SPACE // 2
    chans = tiles.shape[1]
    shaped = tiles.reshape(tile_cols, 2, chans, DZ, TH, TW)
    return shaped.transpose(2, 3, 1, 4, 0, 5).reshape(chans, DZ, 2 * TH, tile_cols * TW)

def split_tiles(volume):
    tile_cols = N_SPACE // 2
    chans = volume.shape[0]
    shaped = volume.reshape(chans, DZ, 2, TH, tile_cols, TW)
    return shaped.transpose(4, 2, 0, 1, 3, 5).reshape(2 * tile_cols, chans, DZ, TH, TW)

def flipped(weights):
    ins, outs = (weights.shape[1], weights.shape[2])
    return weights[::-1].reshape(3, 3, 3, ins, outs).transpose(3, 4, 0, 1, 2)

def transposed_conv(grads, weights):
    padded = jnp.pad(grads, ((0, 0), (1, 1), (1, 1), (1, 1)))
    kernel = flipped(weights).astype(jnp.float32)
    result = lax.conv_general_dilated(padded[None], kernel, (1, 1, 1), 'VALID', dimension_numbers=numbers, precision=lax.Precision.HIGHEST, preferred_element_type=jnp.float32)
    return result[0]

def weight_grad(sources, grads):
    padded = jnp.pad(sources, ((0, 0), (1, 1), (1, 1), (1, 1)))
    depth, rows, width = (grads.shape[1], grads.shape[2], grads.shape[3])
    terms = []
    for kz in range(3):
        for ky in range(3):
            for kx in range(3):
                window = padded[:, kz:kz + depth, ky:ky + rows, kx:kx + width]
                terms.append(jnp.einsum('cdhw,odhw->co', window, grads, precision=lax.Precision.HIGHEST))
    return jnp.stack(terms)

def reference(inputs, pre_act, out_grad, conv1_weight, conv2_weight):

    def one_volume(items):
        input_tiles, act_tiles, slab = items
        volume_in = whole_volume(input_tiles).astype(jnp.float32)
        volume_act = whole_volume(act_tiles).astype(jnp.float32)
        hidden = jnp.where(volume_act > 0, volume_act, leak * volume_act).astype(jnp.bfloat16)
        hidden = lax.optimization_barrier(hidden).astype(jnp.float32)
        grads = slab.transpose(1, 0, 2, 3).astype(jnp.float32)
        hidden_grad = transposed_conv(grads, conv2_weight)
        act_grad = (hidden_grad * jnp.where(volume_act > 0, 1.0, leak)).astype(jnp.bfloat16)
        act_grad = lax.optimization_barrier(act_grad).astype(jnp.float32)
        input_grad = transposed_conv(act_grad, conv1_weight).astype(jnp.bfloat16)
        return (split_tiles(input_grad), weight_grad(hidden, grads), weight_grad(volume_in, act_grad))
    input_grad, second, first = lax.map(one_volume, (inputs, pre_act, out_grad))
    scale = 1.0 / jnp.sqrt(jnp.float32(VOLUMES * DZ * H * W))
    return (input_grad, lax.optimization_barrier(jnp.sum(first, axis=0)) * scale, lax.optimization_barrier(jnp.sum(second, axis=0)) * scale)
```

```python
import functools

import jax
import jax.numpy as jnp
from jax import lax
from jax.experimental import pallas as pl
from jax.experimental.pallas import tpu as pltpu
from jax.sharding import PartitionSpec as P

MESH = pl.DeviceIdType.MESH
leak = 0.3
bf16, f32 = jnp.bfloat16, jnp.float32
NT = (((1,), (1,)), ((), ()))


def log2(n):
    return n.bit_length() - 1


def widen(x, jx):
    if jx == 1:
        return x.astype(bf16)
    lanes = x.shape[1]
    lane = lax.broadcasted_iota(jnp.int32, x.shape, 1)
    x = x.astype(f32)
    if jx == 0:
        return jnp.where(lane == 0, 0.0, pltpu.roll(x, 1, 1)).astype(bf16)
    return jnp.where(lane == lanes - 1, 0.0, pltpu.roll(x, lanes - 1, 1)).astype(bf16)


def flip(bit, me):
    return me + (1 - 2 * ((me // (1 << bit)) % 2)) * (1 << bit)


def kernel(n, ndp, scale, g_ref, p_ref, i_ref, w1_ref, w2_ref,
           o_ref, c1_ref, c2_ref,
           glo, ghi, pbuf, ibuf, s2, s1, b2, b1, hid, alo, ahi, rlo, rhi, d2, d1, obuf, sbuf, rbuf,
           gs, gr, ps, pr, xs, xr, as_, ar, os_, orr, rs, rr_):
    me = lax.axis_index("space")
    dp = lax.axis_index("dp")
    p, rows, C2, W = g_ref.shape
    Zp = p + 2
    C1 = p_ref.shape[2]
    C0 = i_ref.shape[2] // 2
    K2, K1 = 3 * C2, 3 * C1
    cols = W // 128
    pairs = rows // 2
    low, high = (me + n - 1) % n, (me + 1) % n

    barrier = pltpu.get_barrier_semaphore()
    for d in range(1, n):
        pl.semaphore_signal(barrier, inc=1, device_id={"space": (me + d) % n}, device_id_type=MESH)
    for b in range(log2(ndp)):
        pl.semaphore_signal(barrier, inc=1, device_id={"dp": flip(b, dp)}, device_id_type=MESH)
    pl.semaphore_wait(barrier, n - 1 + log2(ndp))

    def remote(src, dst, ss, rsem, where):
        return pltpu.make_async_remote_copy(src_ref=src, dst_ref=dst, send_sem=ss, recv_sem=rsem,
                                            device_id=where, device_id_type=MESH)

    def to_low(src, dst, ss, rsem):
        return remote(src, dst, ss.at[0], rsem.at[0], {"space": low})

    def to_high(src, dst, ss, rsem):
        return remote(src, dst, ss.at[1], rsem.at[1], {"space": high})

    def start_pair(dn, up):
        @pl.when(me > 0)
        def _():
            dn.start()

        @pl.when(me < n - 1)
        def _():
            up.start()

    def wait_pair(dn, up):
        @pl.when(me > 0)
        def _():
            dn.wait_send()
            up.wait_recv()

        @pl.when(me < n - 1)
        def _():
            up.wait_send()
            dn.wait_recv()

    g_dn = to_low(g_ref.at[0], ghi, gs, gr)
    g_up = to_high(g_ref.at[p - 1], glo, gs, gr)
    start_pair(g_dn, g_up)
    p_copies, i_copies = [], []
    for d in range(1, n):
        q = (me + d) % n
        c = remote(p_ref.at[pl.ds(q * p, p)], pbuf.at[me], ps.at[d - 1], pr.at[d - 1], {"space": q})
        c.start()
        p_copies.append(c)
    for d in range(1, n):
        q = (me + d) % n
        c = remote(i_ref.at[pl.ds(q * p, p)], ibuf.at[me], xs.at[d - 1], xr.at[d - 1], {"space": q})
        c.start()
        i_copies.append(c)
    pbuf[me] = p_ref[pl.ds(me * p, p)]
    ibuf[me] = i_ref[pl.ds(me * p, p)]

    b2[...] = jnp.zeros_like(b2)
    b1[...] = jnp.zeros_like(b1)
    for z in range(p):
        for r in range(2):
            for jz in range(3):
                for jy in range(3):
                    at = (r + jy) * Zp + z + jz
                    b2[(z * 2 + r) * C1:(z * 2 + r + 1) * C1, at * K2:(at + 1) * K2] = w2_ref[3 * jz + jy]
                    b1[(z * 2 + r) * C0:(z * 2 + r + 1) * C0, at * K1:(at + 1) * K1] = w1_ref[3 * jz + jy]
    for s, k in ((s2, K2), (s1, K1)):
        s[0:Zp * k, :] = jnp.zeros((Zp * k, W), bf16)
        s[(rows + 1) * Zp * k:(rows + 2) * Zp * k, :] = jnp.zeros((Zp * k, W), bf16)
    d2[...] = jnp.zeros_like(d2)
    d1[...] = jnp.zeros_like(d1)
    sbuf[0] = jnp.zeros(sbuf.shape[1:], f32)

    def spread(s, x, row, zp, chans):
        base = pl.multiple_of(((row + 1) * Zp + zp) * 3 * chans, 16)
        for jx in range(3):
            s[pl.ds(base + jx * chans, chans), :] = widen(x, jx)

    def own(r, carry):
        for z in range(p):
            spread(s2, g_ref[z, r], r, z + 1, C2)
        return carry

    lax.fori_loop(0, rows, own, 0)

    def zero_ends(lo, hi):
        @pl.when(me == 0)
        def _():
            lo[...] = jnp.zeros_like(lo)

        @pl.when(me == n - 1)
        def _():
            hi[...] = jnp.zeros_like(hi)

    zero_ends(glo, ghi)
    wait_pair(g_dn, g_up)

    def halo(r, carry):
        spread(s2, glo[r], r, 0, C2)
        spread(s2, ghi[r], r, p + 1, C2)
        return carry

    lax.fori_loop(0, rows, halo, 0)
    for c in p_copies:
        c.wait()

    def block2(k):
        return s2[pl.ds(pl.multiple_of(k * 2 * Zp * K2, 32), 4 * Zp * K2), :]

    def block1(k):
        return s1[pl.ds(pl.multiple_of(k * 2 * Zp * K1, 32), 4 * Zp * K1), :]

    def first(k, carry):
        hg = jnp.dot(b2[...], block2(k), preferred_element_type=f32)
        for z in range(p):
            for r in range(2):
                m = z * 2 + r
                pre = jnp.concatenate(
                    [pbuf[2 * c + k // 4, z, (2 * k) % 8 + r] for c in range(cols)], axis=1
                ).astype(f32)
                hid[k, m * C1:(m + 1) * C1, :] = jnp.where(pre > 0, pre, leak * pre).astype(bf16)
                part = hg[m * C1:(m + 1) * C1]
                act = (part * jnp.where(pre > 0, 1.0, leak)).astype(bf16)
                spread(s1, act, 2 * k + r, z + 1, C1)
                if z == 0:
                    alo[2 * k + r] = act
                if z == p - 1:
                    ahi[2 * k + r] = act
        return carry

    lax.fori_loop(0, pairs, first, 0)
    a_dn = to_low(alo, rhi, as_, ar)
    a_up = to_high(ahi, rlo, as_, ar)
    start_pair(a_dn, a_up)

    def second(k, carry):
        d2[...] += lax.dot_general(hid[k], block2(k), NT, preferred_element_type=f32)
        return carry

    lax.fori_loop(0, pairs, second, 0)
    for jz in range(3):
        for jy in range(3):
            total = 0.0
            for z in range(p):
                for r in range(2):
                    m, at = z * 2 + r, (r + jy) * Zp + z + jz
                    total += d2[m * C1:(m + 1) * C1, at * K2:(at + 1) * K2]
            j = 3 * jz + jy
            sbuf[0, j * C1:(j + 1) * C1, 0:K2] = total

    zero_ends(rlo, rhi)
    for c in i_copies:
        c.wait()
    wait_pair(a_dn, a_up)

    def halo1(r, carry):
        spread(s1, rlo[r], r, 0, C1)
        spread(s1, rhi[r], r, p + 1, C1)
        return carry

    lax.fori_loop(0, rows, halo1, 0)

    def third(k, carry):
        blk = block1(k)
        ig = jnp.dot(b1[...], blk, preferred_element_type=f32)
        parts = []
        for z in range(p):
            parts.append(jnp.concatenate(
                [ibuf[2 * c + k // 4, z, k % 4].astype(f32) for c in range(cols)], axis=1))
            for c in range(cols):
                obuf[2 * c + k // 4, z, k % 4] = ig[z * 2 * C0:(z + 1) * 2 * C0,
                                                    c * 128:(c + 1) * 128].astype(bf16)
        items = jnp.concatenate(parts, axis=0).astype(bf16)
        d1[...] += lax.dot_general(items, blk, NT, preferred_element_type=f32)
        return carry

    lax.fori_loop(0, pairs, third, 0)
    o_copies = []
    for d in range(1, n):
        q = (me + d) % n
        c = remote(obuf.at[q], o_ref.at[pl.ds(me * p, p)], os_.at[d - 1], orr.at[d - 1], {"space": q})
        c.start()
        o_copies.append(c)
    o_ref[pl.ds(me * p, p)] = obuf[me]
    for jz in range(3):
        for jy in range(3):
            total = 0.0
            for z in range(p):
                for r in range(2):
                    m, at = z * 2 + r, (r + jy) * Zp + z + jz
                    total += d1[m * C0:(m + 1) * C0, at * K1:(at + 1) * K1]
            j = 3 * jz + jy
            sbuf[0, 9 * C1 + j * C0:9 * C1 + (j + 1) * C0, 0:K1] = total

    stages = [("dp", b) for b in range(log2(ndp))] + [("space", b) for b in range(log2(n))]
    for s, (axis, b) in enumerate(stages):
        partner = flip(b, dp if axis == "dp" else me)
        c = remote(sbuf.at[s], rbuf.at[s], rs.at[s], rr_.at[s], {axis: partner})
        c.start()
        c.wait()
        if s < len(stages) - 1:
            sbuf[s + 1] = sbuf[s] + rbuf[s]
    last = len(stages) - 1
    out = (sbuf[last] + rbuf[last]) * scale
    for jz in range(3):
        for jy in range(3):
            for jx in range(3):
                j, k = 3 * jz + jy, 26 - (9 * jz + 3 * jy + jx)
                c2_ref[k] = out[j * C1:(j + 1) * C1, jx * C2:(jx + 1) * C2]
                c1_ref[k] = out[9 * C1 + j * C0:9 * C1 + (j + 1) * C0, jx * C1:(jx + 1) * C1]
    for c in o_copies:
        c.wait()


def body(n, ndp, inputs, pre_act, out_grad, conv1_weight, conv2_weight):
    x, a, g = inputs[0, 0], pre_act[0, 0], out_grad[0]
    C0, DZ, TH, TW = x.shape
    C1 = a.shape[0]
    p, C2, rows, W = g.shape
    Zp = p + 2
    g = g.transpose(0, 2, 1, 3)
    a = a.transpose(1, 2, 0, 3)
    x = x.transpose(1, 2, 0, 3).reshape(DZ, TH // 2, 2 * C0, TW)

    def arrange(w):
        ins, outs = w.shape[1:]
        return w[::-1].reshape(9, 3, ins, outs).transpose(0, 2, 1, 3).reshape(9, ins, 3 * outs)

    K1, K2 = 3 * C1, 3 * C2
    cells = ndp * n * p * rows * W
    nst = log2(n) + log2(ndp)
    red = -(-9 * (C0 + C1) // 8) * 8
    V, D = pltpu.VMEM, pltpu.SemaphoreType.DMA
    vm = pl.BlockSpec(memory_space=pltpu.VMEM)
    o, c1, c2 = pl.pallas_call(
        functools.partial(kernel, n, ndp, float(cells) ** -0.5),
        out_shape=(
            jax.ShapeDtypeStruct((DZ, TH // 2, 2 * C0, TW), bf16),
            jax.ShapeDtypeStruct((27, C0, C1), f32),
            jax.ShapeDtypeStruct((27, C1, C2), f32),
        ),
        in_specs=[vm] * 5,
        out_specs=(vm,) * 3,
        scratch_shapes=[
            V((rows, C2, W), bf16), V((rows, C2, W), bf16),
            V((n, p, TH, C1, TW), bf16), V((n, p, TH // 2, 2 * C0, TW), bf16),
            V(((rows + 2) * Zp * K2, W), bf16), V(((rows + 2) * Zp * K1, W), bf16),
            V((p * 2 * C1, 4 * Zp * K2), bf16), V((p * 2 * C0, 4 * Zp * K1), bf16),
            V((rows // 2, p * 2 * C1, W), bf16),
            V((rows, C1, W), bf16), V((rows, C1, W), bf16), V((rows, C1, W), bf16), V((rows, C1, W), bf16),
            V((p * 2 * C1, 4 * Zp * K2), f32), V((p * 2 * C0, 4 * Zp * K1), f32),
            V((n, p, TH // 2, 2 * C0, TW), bf16),
            V((nst, red, 128), f32), V((nst, red, 128), f32),
            D((2,)), D((2,)), D((n - 1,)), D((n - 1,)), D((n - 1,)), D((n - 1,)), D((2,)), D((2,)),
            D((n - 1,)), D((n - 1,)), D((nst,)), D((nst,)),
        ],
        compiler_params=pltpu.CompilerParams(collective_id=0, has_side_effects=True,
                                             vmem_limit_bytes=56 * 1024 * 1024),
    )(g, a, x, arrange(conv1_weight), arrange(conv2_weight))
    o = o.reshape(DZ, TH, C0, TW).transpose(2, 0, 1, 3)
    return (o[None, None], c1, c2)


def solution(mesh):
    placed = (
        P("dp", "space", None, None, None, None),
        P("dp", "space", None, None, None, None),
        P("dp", "space", None, None, None),
        P(),
        P(),
    )
    return jax.shard_map(
        functools.partial(body, mesh.shape["space"], mesh.shape["dp"]),
        mesh=mesh,
        in_specs=placed,
        out_specs=(P("dp", "space", None, None, None, None), P(), P()),
        check_vma=False,
    )
```

```python
import functools

import jax
import jax.numpy as jnp
from jax import lax
from jax.experimental import pallas as pl
from jax.experimental.pallas import tpu as pltpu
from jax.sharding import PartitionSpec as P

MESH = pl.DeviceIdType.MESH
leak = 0.3
bf16, f32 = jnp.bfloat16, jnp.float32
NT = (((1,), (1,)), ((), ()))


def log2(n):
    return n.bit_length() - 1


def widen(x, jx):
    if jx == 1:
        return x.astype(bf16)
    lanes = x.shape[1]
    lane = lax.broadcasted_iota(jnp.int32, x.shape, 1)
    x = x.astype(f32)
    if jx == 0:
        return jnp.where(lane == 0, 0.0, pltpu.roll(x, 1, 1)).astype(bf16)
    return jnp.where(lane == lanes - 1, 0.0, pltpu.roll(x, lanes - 1, 1)).astype(bf16)


def flip(bit, me):
    return me + (1 - 2 * ((me // (1 << bit)) % 2)) * (1 << bit)


def kernel(n, ndp, scale, g_ref, p_ref, i_ref, w1_ref, w2_ref,
           o_ref, c1_ref, c2_ref,
           glo, ghi, pbuf, ibuf, s2, s1, b2, b1, hid, d2, d1, obuf, otile, osum, w1s, c1s, acc, fin, sbuf, rbuf,
           gs, gr, ps, pr, xs, xr, os_, orr, rs, rr_):
    me = lax.axis_index("space")
    dp = lax.axis_index("dp")
    p, rows, C2, W = g_ref.shape
    Zp = p + 2
    C1 = p_ref.shape[2]
    C0 = i_ref.shape[2] // 2
    K2, K1 = 3 * C2, 3 * C1
    cols = W // 128
    pairs = rows // 2
    low, high = (me + n - 1) % n, (me + 1) % n

    barrier = pltpu.get_barrier_semaphore()
    for d in range(1, n):
        pl.semaphore_signal(barrier, inc=1, device_id={"space": (me + d) % n}, device_id_type=MESH)
    for b in range(log2(ndp)):
        pl.semaphore_signal(barrier, inc=1, device_id={"dp": flip(b, dp)}, device_id_type=MESH)
    pl.semaphore_wait(barrier, n - 1 + log2(ndp))

    def remote(src, dst, ss, rsem, where):
        return pltpu.make_async_remote_copy(src_ref=src, dst_ref=dst, send_sem=ss, recv_sem=rsem,
                                            device_id=where, device_id_type=MESH)

    def to_low(src, dst, ss, rsem):
        return remote(src, dst, ss.at[0], rsem.at[0], {"space": low})

    def to_high(src, dst, ss, rsem):
        return remote(src, dst, ss.at[1], rsem.at[1], {"space": high})

    def start_pair(dn, up):
        @pl.when(me > 0)
        def _():
            dn.start()

        @pl.when(me < n - 1)
        def _():
            up.start()

    def wait_pair(dn, up):
        @pl.when(me > 0)
        def _():
            dn.wait_send()
            up.wait_recv()

        @pl.when(me < n - 1)
        def _():
            up.wait_send()
            dn.wait_recv()

    g_dn = to_low(g_ref.at[0], ghi, gs, gr)
    g_up = to_high(g_ref.at[p - 1], glo, gs, gr)
    start_pair(g_dn, g_up)
    p_copies, i_copies = [], []
    for d in range(1, n):
        q = (me + d) % n
        c = remote(p_ref.at[pl.ds(q * p, p)], pbuf.at[me], ps.at[d - 1], pr.at[d - 1], {"space": q})
        c.start()
        p_copies.append(c)
    for d in range(1, n):
        q = (me + d) % n
        c = remote(i_ref.at[pl.ds(q * p, Zp)], ibuf.at[me], xs.at[d - 1], xr.at[d - 1], {"space": q})
        c.start()
        i_copies.append(c)
    pbuf[me] = p_ref[pl.ds(me * p, p)]
    ibuf[me] = i_ref[pl.ds(me * p, Zp)]

    b2[...] = jnp.zeros_like(b2)
    b1[...] = jnp.zeros_like(b1)
    for c in range(C0):
        w1s[:, c, :] = w1_ref[c].astype(f32).T
    for jz in range(3):
        for jy in range(3):
            ks = [26 - (9 * jz + 3 * jy + jx) for jx in range(3)]
            w2 = jnp.concatenate([w2_ref[k] for k in ks], axis=1)
            w1 = jnp.concatenate([w1s[k] for k in ks], axis=1).astype(bf16)
            for r in range(2):
                for z in range(p):
                    m, at = z * 2 + r, (r + jy) * Zp + z + jz
                    b2[m * C1:(m + 1) * C1, at * K2:(at + 1) * K2] = w2
                for z in range(max(0, 2 - jz), min(Zp, p + 2 - jz)):
                    m, at = z * 2 + r, (r + jy) * p + z - 2 + jz
                    b1[m * C0:(m + 1) * C0, at * K1:(at + 1) * K1] = w1
    for s, k in ((s2, Zp * K2), (s1, p * K1)):
        s[0:k, :] = jnp.zeros((k, W), bf16)
        s[(rows + 1) * k:(rows + 2) * k, :] = jnp.zeros((k, W), bf16)
    d2[...] = jnp.zeros_like(d2)
    d1[...] = jnp.zeros_like(d1)
    acc[...] = jnp.zeros_like(acc)

    def spread(s, x, row, zp, chans, planes):
        base = pl.multiple_of(((row + 1) * planes + zp) * 3 * chans, 16)
        for jx in range(3):
            s[pl.ds(base + jx * chans, chans), :] = widen(x, jx)

    def own(r, carry):
        for z in range(p):
            spread(s2, g_ref[z, r], r, z + 1, C2, Zp)
        return carry

    lax.fori_loop(0, rows, own, 0)

    def zero_ends(lo, hi):
        @pl.when(me == 0)
        def _():
            lo[...] = jnp.zeros_like(lo)

        @pl.when(me == n - 1)
        def _():
            hi[...] = jnp.zeros_like(hi)

    zero_ends(glo, ghi)
    wait_pair(g_dn, g_up)

    def halo(r, carry):
        spread(s2, glo[r], r, 0, C2, Zp)
        spread(s2, ghi[r], r, p + 1, C2, Zp)
        return carry

    lax.fori_loop(0, rows, halo, 0)
    for c in p_copies:
        c.wait()

    def block2(k):
        return s2[pl.ds(pl.multiple_of(k * 2 * Zp * K2, 32), 4 * Zp * K2), :]

    def block1(k):
        return s1[pl.ds(pl.multiple_of(k * 2 * p * K1, 32), 4 * p * K1), :]

    def first(k, carry):
        hg = jnp.dot(b2[...], block2(k), preferred_element_type=f32)
        for z in range(p):
            for r in range(2):
                m = z * 2 + r
                pre = jnp.concatenate(
                    [pbuf[2 * c + k // 4, z, (2 * k) % 8 + r] for c in range(cols)], axis=1
                ).astype(f32)
                hid[k, m * C1:(m + 1) * C1, :] = jnp.where(pre > 0, pre, leak * pre).astype(bf16)
                part = hg[m * C1:(m + 1) * C1]
                act = (part * jnp.where(pre > 0, 1.0, leak)).astype(bf16)
                spread(s1, act, 2 * k + r, z, C1, p)
        return carry

    lax.fori_loop(0, pairs, first, 0)

    for c in i_copies:
        c.wait()

    def third(k, carry):
        blk = block1(k)
        ig = jnp.dot(b1[...], blk, preferred_element_type=f32)
        parts = []
        for z in range(Zp):
            parts.append(jnp.concatenate(
                [ibuf[2 * c + k // 4, z, k % 4].astype(f32) for c in range(cols)], axis=1))
            for c in range(cols):
                obuf[2 * c + k // 4, z, k % 4] = ig[z * 2 * C0:(z + 1) * 2 * C0,
                                                    c * 128:(c + 1) * 128].astype(bf16)
        items = jnp.concatenate(parts, axis=0).astype(bf16)
        d1[...] += lax.dot_general(items, blk, NT, preferred_element_type=f32)
        return carry

    lax.fori_loop(0, pairs, third, 0)
    o_copies = []
    for d in range(1, n):
        q = (me + d) % n
        c = remote(obuf.at[q], otile.at[me], os_.at[d - 1], orr.at[d - 1], {"space": q})
        c.start()
        o_copies.append(c)
    otile[me] = obuf[me]
    def second(k, carry):
        d2[...] += lax.dot_general(hid[k], block2(k), NT, preferred_element_type=f32)
        return carry

    lax.fori_loop(0, pairs, second, 0)
    for jz in range(3):
        for jy in range(3):
            total = 0.0
            for z in range(p):
                for r in range(2):
                    m, at = z * 2 + r, (r + jy) * Zp + z + jz
                    total += d2[m * C1:(m + 1) * C1, at * K2:(at + 1) * K2]
            j = 3 * jz + jy
            acc[j * C1:(j + 1) * C1, 0:K2] = total

    for jz in range(3):
        for jy in range(3):
            total = 0.0
            for z in range(max(0, 2 - jz), min(Zp, p + 2 - jz)):
                for r in range(2):
                    m, at = z * 2 + r, (r + jy) * p + z - 2 + jz
                    total += d1[m * C0:(m + 1) * C0, at * K1:(at + 1) * K1]
            j = 3 * jz + jy
            for jx in range(3):
                acc[(9 * jx + j) * C0:(9 * jx + j + 1) * C0, K2:K2 + C1] = total[:, jx * C1:(jx + 1) * C1]

    half = acc.shape[0] // 2
    core = dp % 2
    mine, other = pl.ds(core * half, half), pl.ds((1 - core) * half, half)
    stages = [("dp", b) for b in range(1, log2(ndp))] + [("space", b) for b in range(log2(n))]
    last = len(stages)
    c = remote(acc.at[other], rbuf.at[last], rs.at[last], rr_.at[last], {"dp": flip(0, dp)})
    c.start()
    c.wait()
    sbuf[0] = acc[mine] + rbuf[last]
    for s, (axis, b) in enumerate(stages):
        partner = flip(b, dp if axis == "dp" else me)
        c = remote(sbuf.at[s], rbuf.at[s], rs.at[s], rr_.at[s], {axis: partner})
        c.start()
        c.wait()
        if s < last - 1:
            sbuf[s + 1] = sbuf[s] + rbuf[s]
    fin[mine] = (sbuf[last - 1] + rbuf[last - 1]) * scale
    f_copy = remote(fin.at[mine], fin.at[mine], rs.at[last + 1], rr_.at[last + 1], {"dp": flip(0, dp)})
    f_copy.start()

    for c in o_copies:
        c.wait()
    for z in range(n * p):
        s, own_z = z // p, z % p
        total = otile[s, own_z + 1].astype(f32)
        if own_z == 0 and s > 0:
            total += otile[s - 1, p + 1].astype(f32)
        if own_z == p - 1 and s < n - 1:
            total += otile[s + 1, 0].astype(f32)
        osum[z] = total.reshape(osum.shape[1:])
        for c in range(C0):
            o_ref[c, z] = osum[z, pl.ds(c, osum.shape[1] // C0, C0), :].astype(bf16)
    f_copy.wait()
    for jz in range(3):
        for jy in range(3):
            for jx in range(3):
                j, k = 3 * jz + jy, 26 - (9 * jz + 3 * jy + jx)
                c2_ref[k] = fin[j * C1:(j + 1) * C1, jx * C2:(jx + 1) * C2]
                c1s[k] = fin[(9 * jx + j) * C0:(9 * jx + j + 1) * C0, K2:K2 + C1]
    for c in range(C0):
        c1_ref[c] = c1s[:, c, :].T


def body(n, ndp, inputs, pre_act, out_grad, conv1_weight, conv2_weight):
    x, a, g = inputs[0, 0], pre_act[0, 0], out_grad[0]
    C0, DZ, TH, TW = x.shape
    C1 = a.shape[0]
    p, C2, rows, W = g.shape
    Zp = p + 2
    g = g.transpose(0, 2, 1, 3)
    a = a.transpose(1, 2, 0, 3)
    x = jnp.pad(x.transpose(1, 2, 0, 3), ((1, 1), (0, 0), (0, 0), (0, 0))).reshape(DZ + 2, TH // 2, 2 * C0, TW)

    K1, K2 = 3 * C1, 3 * C2
    cells = ndp * n * p * rows * W
    nst = log2(n) + log2(ndp)
    red = 9 * C1
    V, D = pltpu.VMEM, pltpu.SemaphoreType.DMA
    vm = pl.BlockSpec(memory_space=pltpu.VMEM)
    o, c1, c2 = pl.pallas_call(
        functools.partial(kernel, n, ndp, float(cells) ** -0.5),
        out_shape=(
            jax.ShapeDtypeStruct((C0, DZ, TH, TW), bf16),
            jax.ShapeDtypeStruct((C0, C1, 27), f32),
            jax.ShapeDtypeStruct((27, C1, C2), f32),
        ),
        in_specs=[vm] * 5,
        out_specs=(vm,) * 3,
        scratch_shapes=[
            V((rows, C2, W), bf16), V((rows, C2, W), bf16),
            V((n, p, TH, C1, TW), bf16), V((n, Zp, TH // 2, 2 * C0, TW), bf16),
            V(((rows + 2) * Zp * K2, W), bf16), V(((rows + 2) * p * K1, W), bf16),
            V((p * 2 * C1, 4 * Zp * K2), bf16), V((Zp * 2 * C0, 4 * p * K1), bf16),
            V((rows // 2, p * 2 * C1, W), bf16),
            V((p * 2 * C1, 4 * Zp * K2), f32), V((Zp * 2 * C0, 4 * p * K1), f32),
            V((n, Zp, TH // 2, 2 * C0, TW), bf16), V((n, Zp, TH // 2, 2 * C0, TW), bf16),
            V((DZ, TH * C0, TW), f32), V((27, C0, C1), f32), V((27, C0, C1), f32),
            V((red, 128), f32), V((red, 128), f32),
            V((nst, red // 2, 128), f32), V((nst, red // 2, 128), f32),
            D((2,)), D((2,)), D((n - 1,)), D((n - 1,)), D((n - 1,)), D((n - 1,)),
            D((n - 1,)), D((n - 1,)), D((nst + 1,)), D((nst + 1,)),
        ],
        compiler_params=pltpu.CompilerParams(collective_id=0, has_side_effects=True,
                                             vmem_limit_bytes=56 * 1024 * 1024),
    )(g, a, x, conv1_weight.transpose(1, 2, 0), conv2_weight)
    return (o[None, None], c1.transpose(2, 0, 1), c2)


def solution(mesh):
    placed = (
        P("dp", "space", None, None, None, None),
        P("dp", "space", None, None, None, None),
        P("dp", "space", None, None, None),
        P(),
        P(),
    )
    return jax.shard_map(
        functools.partial(body, mesh.shape["space"], mesh.shape["dp"]),
        mesh=mesh,
        in_specs=placed,
        out_specs=(P("dp", "space", None, None, None, None), P(), P()),
        check_vma=False,
    )
```

```python
import functools

import jax
import jax.numpy as jnp
from jax import lax
from jax.experimental import pallas as pl
from jax.experimental.pallas import tpu as pltpu
from jax.sharding import PartitionSpec as P

MESH = pl.DeviceIdType.MESH
leak = 0.3
bf16, f32 = jnp.bfloat16, jnp.float32
NT = (((1,), (1,)), ((), ()))


def log2(n):
    return n.bit_length() - 1


def widen(x, jx):
    if jx == 1:
        return x.astype(bf16)
    lanes = x.shape[1]
    lane = lax.broadcasted_iota(jnp.int32, x.shape, 1)
    x = x.astype(f32)
    if jx == 0:
        return jnp.where(lane == 0, 0.0, pltpu.roll(x, 1, 1)).astype(bf16)
    return jnp.where(lane == lanes - 1, 0.0, pltpu.roll(x, lanes - 1, 1)).astype(bf16)


def flip(bit, me):
    return me + (1 - 2 * ((me // (1 << bit)) % 2)) * (1 << bit)


def kernel(n, ndp, scale, g_ref, p_ref, i_ref, w1_ref, w2_ref,
           o_ref, c1_ref, c2_ref,
           glo, ghi, pbuf, ibuf, s2, s1, b2, b1, hid, d2, d1, obuf, otile, osum, w1s, c1s, acc, fin, sbuf, rbuf,
           gs, gr, ps, pr, xs, xr, os_, orr, rs, rr_):
    me = lax.axis_index("space")
    dp = lax.axis_index("dp")
    p, rows, C2, W = g_ref.shape
    Zp = p + 2
    C1 = p_ref.shape[2]
    C0 = i_ref.shape[2] // 2
    K2, K1 = 3 * C2, 3 * C1
    cols = W // 128
    pairs = rows // 2
    low, high = (me + n - 1) % n, (me + 1) % n

    barrier = pltpu.get_barrier_semaphore()
    for d in range(1, n):
        pl.semaphore_signal(barrier, inc=1, device_id={"space": (me + d) % n}, device_id_type=MESH)
    for b in range(log2(ndp)):
        pl.semaphore_signal(barrier, inc=1, device_id={"dp": flip(b, dp)}, device_id_type=MESH)
    pl.semaphore_wait(barrier, n - 1 + log2(ndp))

    def remote(src, dst, ss, rsem, where):
        return pltpu.make_async_remote_copy(src_ref=src, dst_ref=dst, send_sem=ss, recv_sem=rsem,
                                            device_id=where, device_id_type=MESH)

    def to_low(src, dst, ss, rsem):
        return remote(src, dst, ss.at[0], rsem.at[0], {"space": low})

    def to_high(src, dst, ss, rsem):
        return remote(src, dst, ss.at[1], rsem.at[1], {"space": high})

    def start_pair(dn, up):
        @pl.when(me > 0)
        def _():
            dn.start()

        @pl.when(me < n - 1)
        def _():
            up.start()

    def wait_pair(dn, up):
        @pl.when(me > 0)
        def _():
            dn.wait_send()
            up.wait_recv()

        @pl.when(me < n - 1)
        def _():
            up.wait_send()
            dn.wait_recv()

    g_dn = to_low(g_ref.at[0], ghi, gs, gr)
    g_up = to_high(g_ref.at[p - 1], glo, gs, gr)
    p_copies, i_copies = [], []
    for d in range(1, n):
        q = (me + d) % n
        c = remote(p_ref.at[pl.ds(q * p, p)], pbuf.at[me], ps.at[d - 1], pr.at[d - 1], {"space": q})
        c.start()
        p_copies.append(c)
    start_pair(g_dn, g_up)
    for d in range(1, n):
        q = (me + d) % n
        c = remote(i_ref.at[pl.ds(q * p, Zp)], ibuf.at[me], xs.at[d - 1], xr.at[d - 1], {"space": q})
        c.start()
        i_copies.append(c)
    pbuf[me] = p_ref[pl.ds(me * p, p)]
    ibuf[me] = i_ref[pl.ds(me * p, Zp)]

    b2[...] = jnp.zeros_like(b2)
    b1[...] = jnp.zeros_like(b1)
    for c in range(C0):
        w1s[:, c, :] = w1_ref[c].astype(f32).T
    for jz in range(3):
        for jy in range(3):
            ks = [26 - (9 * jz + 3 * jy + jx) for jx in range(3)]
            w2 = jnp.concatenate([w2_ref[k] for k in ks], axis=1)
            w1 = jnp.concatenate([w1s[k] for k in ks], axis=1).astype(bf16)
            for r in range(2):
                for z in range(p):
                    m, at = z * 2 + r, (r + jy) * Zp + z + jz
                    b2[m * C1:(m + 1) * C1, at * K2:(at + 1) * K2] = w2
                for z in range(max(0, 2 - jz), min(Zp, p + 2 - jz)):
                    m, at = z * 2 + r, (r + jy) * p + z - 2 + jz
                    b1[m * C0:(m + 1) * C0, at * K1:(at + 1) * K1] = w1
    for s, k in ((s2, Zp * K2), (s1, p * K1)):
        s[0:k, :] = jnp.zeros((k, W), bf16)
        s[(rows + 1) * k:(rows + 2) * k, :] = jnp.zeros((k, W), bf16)
    d2[...] = jnp.zeros_like(d2)
    d1[...] = jnp.zeros_like(d1)
    acc[...] = jnp.zeros_like(acc)

    def spread(s, x, row, zp, chans, planes):
        base = pl.multiple_of(((row + 1) * planes + zp) * 3 * chans, 16)
        for jx in range(3):
            s[pl.ds(base + jx * chans, chans), :] = widen(x, jx)

    def own(r, carry):
        for z in range(p):
            spread(s2, g_ref[z, r], r, z + 1, C2, Zp)
        return carry

    lax.fori_loop(0, rows, own, 0, unroll=4)

    def zero_ends(lo, hi):
        @pl.when(me == 0)
        def _():
            lo[...] = jnp.zeros_like(lo)

        @pl.when(me == n - 1)
        def _():
            hi[...] = jnp.zeros_like(hi)

    zero_ends(glo, ghi)
    wait_pair(g_dn, g_up)

    def halo(r, carry):
        spread(s2, glo[r], r, 0, C2, Zp)
        spread(s2, ghi[r], r, p + 1, C2, Zp)
        return carry

    lax.fori_loop(0, rows, halo, 0, unroll=4)
    for c in p_copies:
        c.wait()

    def block2(k):
        return s2[pl.ds(pl.multiple_of(k * 2 * Zp * K2, 32), 4 * Zp * K2), :]

    def block1(k):
        return s1[pl.ds(pl.multiple_of(k * 2 * p * K1, 32), 4 * p * K1), :]

    def first(k, carry):
        hg = jnp.dot(b2[...], block2(k), preferred_element_type=f32)
        for z in range(p):
            for r in range(2):
                m = z * 2 + r
                pre = jnp.concatenate(
                    [pbuf[2 * c + k // 4, z, (2 * k) % 8 + r] for c in range(cols)], axis=1
                ).astype(f32)
                hid[k, m * C1:(m + 1) * C1, :] = jnp.where(pre > 0, pre, leak * pre).astype(bf16)
                part = hg[m * C1:(m + 1) * C1]
                act = (part * jnp.where(pre > 0, 1.0, leak)).astype(bf16)
                spread(s1, act, 2 * k + r, z, C1, p)
        return carry

    lax.fori_loop(0, pairs, first, 0, unroll=4)

    for c in i_copies:
        c.wait()

    def third(k, carry):
        blk = block1(k)
        ig = jnp.dot(b1[...], blk, preferred_element_type=f32)
        parts = []
        for z in range(Zp):
            parts.append(jnp.concatenate(
                [ibuf[2 * c + k // 4, z, k % 4].astype(f32) for c in range(cols)], axis=1))
            for c in range(cols):
                obuf[2 * c + k // 4, z, k % 4] = ig[z * 2 * C0:(z + 1) * 2 * C0,
                                                    c * 128:(c + 1) * 128]
        items = jnp.concatenate(parts, axis=0).astype(bf16)
        d1[...] += lax.dot_general(items, blk, NT, preferred_element_type=f32)
        return carry

    lax.fori_loop(0, pairs, third, 0, unroll=4)
    o_copies = []
    for d in range(1, n):
        q = (me + d) % n
        c = remote(obuf.at[q], otile.at[me], os_.at[d - 1], orr.at[d - 1], {"space": q})
        c.start()
        o_copies.append(c)
    otile[me] = obuf[me]
    def second(k, carry):
        d2[...] += lax.dot_general(hid[k], block2(k), NT, preferred_element_type=f32)
        return carry

    lax.fori_loop(0, pairs, second, 0, unroll=4)
    for jz in range(3):
        for jy in range(3):
            total = 0.0
            for z in range(p):
                for r in range(2):
                    m, at = z * 2 + r, (r + jy) * Zp + z + jz
                    total += d2[m * C1:(m + 1) * C1, at * K2:(at + 1) * K2]
            j = 3 * jz + jy
            acc[j * C1:(j + 1) * C1, 0:K2] = total

    for jz in range(3):
        for jy in range(3):
            total = 0.0
            for z in range(max(0, 2 - jz), min(Zp, p + 2 - jz)):
                for r in range(2):
                    m, at = z * 2 + r, (r + jy) * p + z - 2 + jz
                    total += d1[m * C0:(m + 1) * C0, at * K1:(at + 1) * K1]
            j = 3 * jz + jy
            for jx in range(3):
                acc[(9 * jx + j) * C0:(9 * jx + j + 1) * C0, K2:K2 + C1] = total[:, jx * C1:(jx + 1) * C1]

    def assemble():
        for c in o_copies:
            c.wait()
        for z in range(n * p):
            s, own_z = z // p, z % p
            total = otile[s, own_z + 1].astype(f32)
            if own_z == 0 and s > 0:
                total += otile[s - 1, p + 1].astype(f32)
            if own_z == p - 1 and s < n - 1:
                total += otile[s + 1, 0].astype(f32)
            osum[z] = total.reshape(osum.shape[1:])
            for c in range(C0):
                o_ref[c, z] = osum[z, pl.ds(c, osum.shape[1] // C0, C0), :].astype(bf16)

    half = acc.shape[0] // 2
    core = dp % 2
    mine, other = pl.ds(core * half, half), pl.ds((1 - core) * half, half)
    stages = [("dp", b) for b in range(1, log2(ndp))] + [("space", b) for b in range(log2(n))]
    last = len(stages)
    c = remote(acc.at[other], rbuf.at[last], rs.at[last], rr_.at[last], {"dp": flip(0, dp)})
    c.start()
    c.wait()
    sbuf[0] = acc[mine] + rbuf[last]
    for s, (axis, b) in enumerate(stages):
        partner = flip(b, dp if axis == "dp" else me)
        c = remote(sbuf.at[s], rbuf.at[s], rs.at[s], rr_.at[s], {axis: partner})
        c.start()
        if s == last - 1:
            assemble()
        c.wait()
        if s < last - 1:
            sbuf[s + 1] = sbuf[s] + rbuf[s]
    fin[mine] = (sbuf[last - 1] + rbuf[last - 1]) * scale
    f_copy = remote(fin.at[mine], fin.at[mine], rs.at[last + 1], rr_.at[last + 1], {"dp": flip(0, dp)})
    f_copy.start()

    f_copy.wait()
    for jz in range(3):
        for jy in range(3):
            for jx in range(3):
                j, k = 3 * jz + jy, 26 - (9 * jz + 3 * jy + jx)
                c2_ref[k] = fin[j * C1:(j + 1) * C1, jx * C2:(jx + 1) * C2]
                c1s[k] = fin[(9 * jx + j) * C0:(9 * jx + j + 1) * C0, K2:K2 + C1]
    for c in range(C0):
        c1_ref[c] = c1s[:, c, :].T


def body(n, ndp, inputs, pre_act, out_grad, conv1_weight, conv2_weight):
    x, a, g = inputs[0, 0], pre_act[0, 0], out_grad[0]
    C0, DZ, TH, TW = x.shape
    C1 = a.shape[0]
    p, C2, rows, W = g.shape
    Zp = p + 2
    g = g.transpose(0, 2, 1, 3)
    a = a.transpose(1, 2, 0, 3)
    x = jnp.pad(x.transpose(1, 2, 0, 3), ((1, 1), (0, 0), (0, 0), (0, 0))).reshape(DZ + 2, TH // 2, 2 * C0, TW)

    K1, K2 = 3 * C1, 3 * C2
    cells = ndp * n * p * rows * W
    nst = log2(n) + log2(ndp)
    red = 9 * C1
    V, D = pltpu.VMEM, pltpu.SemaphoreType.DMA
    vm = pl.BlockSpec(memory_space=pltpu.VMEM)
    o, c1, c2 = pl.pallas_call(
        functools.partial(kernel, n, ndp, float(cells) ** -0.5),
        out_shape=(
            jax.ShapeDtypeStruct((C0, DZ, TH, TW), bf16),
            jax.ShapeDtypeStruct((C0, C1, 27), f32),
            jax.ShapeDtypeStruct((27, C1, C2), f32),
        ),
        in_specs=[vm] * 5,
        out_specs=(vm,) * 3,
        scratch_shapes=[
            V((rows, C2, W), bf16), V((rows, C2, W), bf16),
            V((n, p, TH, C1, TW), bf16), V((n, Zp, TH // 2, 2 * C0, TW), bf16),
            V(((rows + 2) * Zp * K2, W), bf16), V(((rows + 2) * p * K1, W), bf16),
            V((p * 2 * C1, 4 * Zp * K2), bf16), V((Zp * 2 * C0, 4 * p * K1), bf16),
            V((rows // 2, p * 2 * C1, W), bf16),
            V((p * 2 * C1, 4 * Zp * K2), f32), V((Zp * 2 * C0, 4 * p * K1), f32),
            V((n, Zp, TH // 2, 2 * C0, TW), f32), V((n, Zp, TH // 2, 2 * C0, TW), f32),
            V((DZ, TH * C0, TW), f32), V((27, C0, C1), f32), V((27, C0, C1), f32),
            V((red, 128), f32), V((red, 128), f32),
            V((nst, red // 2, 128), f32), V((nst, red // 2, 128), f32),
            D((2,)), D((2,)), D((n - 1,)), D((n - 1,)), D((n - 1,)), D((n - 1,)),
            D((n - 1,)), D((n - 1,)), D((nst + 1,)), D((nst + 1,)),
        ],
        compiler_params=pltpu.CompilerParams(collective_id=0, has_side_effects=True,
                                             vmem_limit_bytes=56 * 1024 * 1024),
    )(g, a, x, conv1_weight.transpose(1, 2, 0), conv2_weight)
    return (o[None, None], c1.transpose(2, 0, 1), c2)


def solution(mesh):
    placed = (
        P("dp", "space", None, None, None, None),
        P("dp", "space", None, None, None, None),
        P("dp", "space", None, None, None),
        P(),
        P(),
    )
    return jax.shard_map(
        functools.partial(body, mesh.shape["space"], mesh.shape["dp"]),
        mesh=mesh,
        in_specs=placed,
        out_specs=(P("dp", "space", None, None, None, None), P(), P()),
        check_vma=False,
    )
```
